32 devices in a mesh: slab: 8 (over z, core), split: 4 (over y, x).
Axes of the slice: x: 2, y: 2, z: 4, core: 2. Of those that a mesh axis runs over, the one named last changes fastest.
Arguments:
- displacement: float32 [3, 64, 128, 256], P(None, 'slab', 'split'), may hold values from -0.3 to 0.3
- velocity: float32 [3, 64, 128, 256], P(None, 'slab', 'split'), may hold values from -0.6 to 0.6
- acceleration: float32 [3, 64, 128, 256], P(None, 'slab', 'split'), may hold values from -1.8 to 1.8
- bond_masks: int32 [4, 64, 128, 256], P(None, 'slab', 'split'), may hold values from 0 to 255, as said below
- proj_pos: float32 [32, 3, 128], replicated, may hold values from -0.5 to 257, as said below
- proj_vel: float32 [32, 3, 128], replicated, may hold values from -1.8 to 1.8
- proj_acc: float32 [32, 3, 128], replicated, may hold values from -1.8 to 1.8
- contact_pairs: int32 [3, 2, 512], P(None, None, ('slab', 'split')), may hold values from -1 to 31, as said below
Outputs:
- final_displacement: float32 [3, 64, 128, 256], P(None, 'slab', 'split')
- final_velocity: float32 [3, 64, 128, 256], P(None, 'slab', 'split')
- final_proj_pos: float32 [32, 3, 128], replicated
- final_proj_vel: float32 [32, 3, 128], replicated
The draws below stay inside these ranges and needn't reach their ends.
Inputs may be any that keep to these rules, and one draw needn't show every extreme that they name: `bond_masks`: bit b of word w (the value divided by 2 to the b, modulo 2) is 1 where the bond from the cell to the offset numbered 8 w + b is intact. `contact_pairs`: slots d * 16 to (d + 1) * 16 - 1 belong to device d. Row 0 names one of that device's 8 surface blocks; row 1 names a projectile block, or -1 for an empty slot. Live slots come first on every device and no pair repeats on a device within a substep. In every substep each projectile block is paired on exactly one device, one of the four devices of the 2 x 2 group of device blocks under it, and on another device than in the substep before; in every substep some device has all 16 slots live. `proj_pos`: the device blocks fall into 2 x 2 groups (slab indices 2a and 2a + 1, split indices 2b and 2b + 1). Every projectile block lies above one such group, between 0.5 and 2 cells over the top layer, and every group lies under exactly 4 projectile blocks.
All inputs are finite; a program needn't handle non-finite values.
Results may differ from the reference program's by a relative error of at most 0.0003.
Values sent between devices are 32-bit elements; how exact they have to be, the bound alone decides.
A program may use at most 128 MiB of HBM per device.

```python
import math
import jax
import jax.numpy as jnp
from jax import lax

CX = 8
CY = 32
NZ = 256
SUB = 3
SL = 4
PTS = 128
MAXH = 4
NX = 64
NY = 128
SB_DEV = 8
TPB = 4
MAXP = 16
PB = 32
N_SPLIT = 4


def quad_owners(key):
    base_key = jax.random.fold_in(key, 7)
    keys = jax.random.split(base_key, 6)
    slab_count = NX // CX
    split_count = NY // CY
    devices = slab_count * split_count
    quad_count = devices // 4
    half_split = split_count // 2
    per_quad = PB // quad_count
    quad_of = jax.random.permutation(keys[0], (jnp.arange(PB) // per_quad).astype(jnp.int32)).astype(jnp.int32)
    center = jax.random.randint(keys[1], (), 0, quad_count)
    in_center = quad_of == center
    own_start = jax.random.randint(keys[2], (PB,), 0, 4)
    own_steps = jax.random.randint(keys[3], (SUB, PB), 1, 4)
    common_start = jax.random.randint(keys[4], (), 0, 4)
    common_steps = jax.random.randint(keys[5], (SUB, 1), 1, 4)
    corner = jnp.where(in_center, common_start, own_start).astype(jnp.int32)
    step_sizes = jnp.where(in_center[None, :], common_steps, own_steps).astype(jnp.int32)
    owner_rows = []
    for substep in range(SUB):
        if substep > 0:
            corner = (corner + step_sizes[substep]) % 4
        row_index = 2 * (quad_of // half_split) + corner // 2
        column_index = 2 * (quad_of % half_split) + corner % 2
        owner_rows.append((row_index * split_count + column_index).astype(jnp.int32))
    return (quad_of, jnp.stack(owner_rows))


def draw_bond_masks(key, part):
    mask_key = jax.random.fold_in(key, 41)
    packed = jnp.zeros((4, NX, NY, NZ), jnp.int32)
    for bit_index in range(8):
        digits = jax.random.randint(jax.random.fold_in(mask_key, bit_index), (4, NX, NY, NZ), 0, 5)
        packed = packed + (digits < 4).astype(jnp.int32) * 2 ** bit_index
    return packed


def draw_contact_pairs(key, part):
    quad_of, owners = quad_owners(key)
    devices = NX // CX * (NY // CY)
    indices = jnp.arange(PB).astype(jnp.int32)
    earlier = (owners[:, None, :] == owners[:, :, None]) & (indices[None, None, :] < indices[None, :, None])
    owner_rank = jnp.sum(earlier.astype(jnp.int32), axis=2)
    step_index = jnp.broadcast_to(jnp.arange(SUB).astype(jnp.int32)[:, None], (SUB, PB))
    block_index = jnp.broadcast_to(indices[None, :], (SUB, PB))
    home_table = jnp.full((SUB, devices, MAXH), -1, jnp.int32).at[step_index, owners, owner_rank].set(block_index)
    slot_keys = jax.random.split(jax.random.fold_in(key, 13), SUB * devices * MAXH)
    target_picks = jax.vmap(lambda slot_key: jax.random.permutation(slot_key, SB_DEV)[:TPB])(slot_keys)
    targets = target_picks.reshape(SUB, devices * MAXH * TPB).astype(jnp.int32)
    chosen = jnp.broadcast_to(home_table[:, :, :, None], (SUB, devices, MAXH, TPB)).reshape(SUB, devices * MAXH * TPB)
    return jnp.stack([targets, chosen.astype(jnp.int32)], axis=1)


def draw_proj_pos(key, part):
    quad_of, owners = quad_owners(key)
    half_split = NY // CY // 2
    base_x = (quad_of // half_split * 2 * CX).astype(jnp.float32)
    base_y = (quad_of % half_split * 2 * CY).astype(jnp.float32)
    float_keys = jax.random.split(jax.random.fold_in(key, 29), 3)
    along_x = base_x[:, None] + jax.random.uniform(float_keys[0], (PB, PTS), jnp.float32, -0.5, 2 * CX - 0.5)
    along_y = base_y[:, None] + jax.random.uniform(float_keys[1], (PB, PTS), jnp.float32, -0.5, 2 * CY - 0.5)
    height = NZ - 1 + jax.random.uniform(float_keys[2], (PB, PTS), jnp.float32, 0.5, 2.0)
    return jnp.stack([along_x, along_y, height], axis=1)


def level_of(stream_key, shape, cuts, smallest, high):
    def one(dim, blocks):
        draws = jax.random.uniform(jax.random.fold_in(jax.random.fold_in(stream_key, 6), dim), (blocks,), jnp.float32, smallest / len(cuts), high / len(cuts))
        return jnp.repeat(jnp.exp(draws), shape[dim] // blocks).reshape((-1,) + (1,) * (len(shape) - dim - 1))

    factor_of = one(*cuts[0])
    for cut in cuts[1:]:
        factor_of = factor_of * one(*cut)
    return factor_of


def normal_values(stream_key, dims, width, bound, cuts=(), kind=jnp.bfloat16):
    level = level_of(stream_key, dims, cuts, -0.22, 0.18) if cuts else 1.0
    entries = jax.random.normal(stream_key, dims, jnp.float32) * width * level
    return jnp.minimum(jnp.maximum(entries, -bound), bound).astype(kind)


def setup_inputs(seed: int = 0) -> dict:
    arg_keys = jax.random.split(jax.random.key(seed), 9)
    return {
        "displacement": normal_values(arg_keys[0], (3, NX, NY, NZ), 0.05, 0.3, ((1, 8), (2, 4)), jnp.float32),
        "velocity": normal_values(arg_keys[1], (3, NX, NY, NZ), 0.1, 0.6, ((1, 8), (2, 4)), jnp.float32),
        "acceleration": normal_values(arg_keys[2], (3, NX, NY, NZ), 0.3, 1.8, ((1, 8), (2, 4)), jnp.float32),
        "bond_masks": draw_bond_masks(jax.random.fold_in(arg_keys[8], 71), 0),
        "proj_pos": draw_proj_pos(jax.random.fold_in(arg_keys[8], 71), 0),
        "proj_vel": normal_values(arg_keys[5], (PB, 3, PTS), 0.3, 1.8, (), jnp.float32),
        "proj_acc": normal_values(arg_keys[6], (PB, 3, PTS), 0.3, 1.8, (), jnp.float32),
        "contact_pairs": draw_contact_pairs(jax.random.fold_in(arg_keys[8], 71), 0),
    }


time_step = 0.25
bond_stiffness = 0.5
contact_stiffness = 0.05
contact_width = 8.0
inverse_mass = 0.5

def bond_offsets():
    listed = []
    for shift_x in (-2, -1, 0, 1, 2):
        for shift_y in (-2, -1, 0, 1, 2):
            for shift_z in (-2, -1, 0, 1, 2):
                squared = shift_x * shift_x + shift_y * shift_y + shift_z * shift_z
                if 0 < squared <= 4:
                    listed.append((shift_x, shift_y, shift_z))
    return listed

def bond_term(neighbour, displace, intact, valid_bond, offset):
    shift_x, shift_y, shift_z = offset
    length = math.sqrt(shift_x * shift_x + shift_y * shift_y + shift_z * shift_z)
    along_x = shift_x + (neighbour[0] - displace[0])
    along_y = shift_y + (neighbour[1] - displace[1])
    along_z = shift_z + (neighbour[2] - displace[2])
    squared = along_x * along_x + along_y * along_y + along_z * along_z
    stretch = (squared - length * length) / (length * (jnp.sqrt(squared) + length))
    return bond_stiffness / length * stretch * intact * valid_bond

def add_bond(bond_total, coefficient, offset):
    direction = jnp.array(offset, bond_total.dtype)
    return bond_total + direction[:, None, None, None] * coefficient[None]

def bond_forces(displace, mask_words):
    padded = jnp.pad(displace, ((0, 0), (2, 2), (2, 2), (2, 2)))
    inside_x = jnp.pad(jnp.ones((NX,), displace.dtype), 2)
    inside_y = jnp.pad(jnp.ones((NY,), displace.dtype), 2)
    inside_z = jnp.pad(jnp.ones((NZ,), displace.dtype), 2)
    bond_total = jnp.zeros_like(displace)
    for number, offset in enumerate(bond_offsets()):
        shift_x, shift_y, shift_z = offset
        neighbour = padded[:, 2 + shift_x:2 + shift_x + NX, 2 + shift_y:2 + shift_y + NY, 2 + shift_z:2 + shift_z + NZ]
        valid_bond = inside_x[2 + shift_x:2 + shift_x + NX][:, None, None] * inside_y[2 + shift_y:2 + shift_y + NY][None, :, None] * inside_z[2 + shift_z:2 + shift_z + NZ][None, None, :]
        intact = (mask_words[number // 8] // 2 ** (number % 8) % 2).astype(displace.dtype)
        bond_total = add_bond(bond_total, bond_term(neighbour, displace, intact, valid_bond, offset), offset)
    return bond_total

def contact_tile(points, particles):
    separation = points[:, :, None] - particles[:, None, :]
    squared = lax.optimization_barrier(jnp.sum(separation * separation, axis=0))
    weight = contact_stiffness * jnp.exp(-squared / contact_width)
    pulled = weight[None] * separation
    return (lax.optimization_barrier(jnp.sum(pulled, axis=2)), -lax.optimization_barrier(jnp.sum(pulled, axis=1)))

def contact_forces(displace, positions, slot_pairs):
    anchor = jnp.zeros((), jnp.int32)
    lattice = jnp.stack([jnp.broadcast_to(jnp.arange(NX).astype(displace.dtype)[:, None, None], (NX, NY, SL)), jnp.broadcast_to(jnp.arange(NY).astype(displace.dtype)[None, :, None], (NX, NY, SL)), jnp.broadcast_to((NZ - SL + jnp.arange(SL)).astype(displace.dtype)[None, None, :], (NX, NY, SL))])
    places = displace[:, :, :, NZ - SL:] + lattice

    def visit(running, slot_index):
        surface_force, particle_force = running
        device = slot_index // MAXP
        corner_x = (device // N_SPLIT * CX).astype(jnp.int32)
        corner_y = (device % N_SPLIT * CY).astype(jnp.int32)
        starts = (anchor, corner_x, corner_y, anchor)
        region = lax.dynamic_slice(places, starts, (3, CX, CY, SL)).reshape(3, SB_DEV, PTS)
        surface_block = slot_pairs[0, slot_index]
        chosen = slot_pairs[1, slot_index]
        is_live = (chosen >= 0).astype(places.dtype)
        picked = jnp.maximum(chosen, 0)
        on_points, on_particles = contact_tile(region[:, surface_block], positions[picked])
        patch_force = jnp.zeros((3, SB_DEV, PTS), places.dtype).at[:, surface_block].set(on_points * is_live)
        current = lax.dynamic_slice(surface_force, starts, (3, CX, CY, SL))
        surface_force = lax.dynamic_update_slice(surface_force, current + patch_force.reshape(3, CX, CY, SL), starts)
        particle_force = particle_force.at[picked].add(on_particles * is_live)
        return ((surface_force, particle_force), None)
    initial = (jnp.zeros_like(places), jnp.zeros_like(positions))
    finals, ignored = lax.scan(visit, initial, jnp.arange(slot_pairs.shape[1]).astype(jnp.int32))
    return finals

def reference(displacement, velocity, acceleration, bond_masks, proj_pos, proj_vel, proj_acc, contact_pairs):
    for substep in range(SUB):
        half_velocity = velocity + 0.5 * time_step * acceleration
        displacement = displacement + time_step * half_velocity
        proj_half = proj_vel + 0.5 * time_step * proj_acc
        proj_pos = proj_pos + time_step * proj_half
        forces = bond_forces(displacement, bond_masks)
        surface_force, particle_force = contact_forces(displacement, proj_pos, contact_pairs[substep])
        forces = forces + jnp.pad(surface_force, ((0, 0), (0, 0), (0, 0), (NZ - SL, 0)))
        acceleration = forces
        velocity = half_velocity + 0.5 * time_step * acceleration
        proj_acc = inverse_mass * particle_force
        proj_vel = proj_half + 0.5 * time_step * proj_acc
    return (displacement, velocity, proj_pos, proj_vel)
```

```python
import functools
import math

import jax
import jax.numpy as jnp
from jax import lax
from jax.experimental import pallas as pl
from jax.experimental.pallas import tpu as pltpu
from jax.sharding import PartitionSpec as P

SL = 4
PTS = 128
SB_DEV = 8
LANES = 128

time_step = 0.25
bond_stiffness = 0.5
contact_stiffness = 0.05
contact_width = 8.0
inverse_mass = 0.5
tiny = 1e-30
MESH = pl.DeviceIdType.MESH


def bond_offsets():
    listed = []
    for shift_x in (-2, -1, 0, 1, 2):
        for shift_y in (-2, -1, 0, 1, 2):
            for shift_z in (-2, -1, 0, 1, 2):
                squared = shift_x * shift_x + shift_y * shift_y + shift_z * shift_z
                if 0 < squared <= 4:
                    listed.append((shift_x, shift_y, shift_z))
    return listed


OFFSETS = bond_offsets()
CORNERS = [(-1, -1), (-1, 1), (1, -1), (1, 1)]
SIDES = [(-1, 0), (1, 0), (0, -1), (0, 1)]


def kernel(
    dims,
    targets_ref, slots_ref, inverse_ref, mine_ref, place_ref,
    disp_ref, vel_ref, acc_ref, mask_ref, qpos_ref, qvel_ref, qacc_ref,
    out_disp, out_vel, out_pos, out_pvel,
    u_0, u_p, u_m, u_pp, u_mm, force, factors, edges_y, edges_c,
    got_x, got_y, got_c, wide, slot_point, slot_part, qp, qv, qa, rel,
    part_send, part_got, fin, gathered,
    send_x, recv_x, send_y, recv_y, send_c, recv_c, send_p, recv_p, send_g, recv_g,
):
    subs, nx, ny, nz, slabs, splits, per_group, blocks = dims
    halves = nz // LANES
    tiles = ny // 8
    slots = slots_ref.shape[0] // subs
    top = halves - 1
    me_x = lax.axis_index("slab")
    me_y = lax.axis_index("split")
    mid_x, mid_y = nx // 2, ny // 2
    half_split = splits // 2
    groups = (slabs // 2) * half_split
    my_group = (me_x // 2) * half_split + me_y // 2
    my_x, my_y = lax.rem(me_x, 2), lax.rem(me_y, 2)
    my_id = my_x * 2 + my_y

    def exists(dx, dy):
        ok = None
        for d, me, n in ((dx, me_x, slabs), (dy, me_y, splits)):
            if d:
                cond = (me > 0) if d < 0 else (me < n - 1)
                ok = cond if ok is None else ok & cond
        return ok

    barrier = pltpu.get_barrier_semaphore()

    def greet(x, y):
        pl.semaphore_signal(barrier, inc=1, device_id=(x, y), device_id_type=MESH)

    for dx, dy in SIDES + CORNERS:
        @pl.when(exists(dx, dy))
        def _():
            greet(me_x + dx, me_y + dy)

    def group_xy(g):
        return 2 * (g // half_split) + my_x, 2 * lax.rem(g, half_split) + my_y

    @pl.loop(0, groups)
    def _(g):
        @pl.when(g != my_group)
        def _():
            x, y = group_xy(g)
            greet(x, y)

    lane = lax.broadcasted_iota(jnp.int32, (8, LANES), 1)
    row8 = lax.broadcasted_iota(jnp.int32, (8, LANES), 0)

    zero_tile = jnp.zeros((8, LANES), jnp.float32)
    for ref in (u_0, u_p, u_m):
        for x in (0, 1, nx + 2, nx + 3):
            ref[:, x] = jnp.zeros(ref.shape[:1] + ref.shape[2:], jnp.float32)

        @pl.loop(2, nx + 2)
        def _(x):
            for c in range(3):
                for h in range(halves):
                    ref[c, x, h, 0:8, :] = zero_tile
                    ref[c, x, h, ny + 8 : ny + 16, :] = zero_tile

    @pl.loop(0, nx)
    def _(x):
        at_x = me_x * nx + x
        ok_x = {
            d: jnp.where((at_x + d >= 0) & (at_x + d < slabs * nx), 1.0, 0.0)
            for d in (-2, -1, 0, 1, 2)
        }
        for h in range(halves):
            at_z = lane + h * LANES
            ok_z = {d: (at_z + d >= 0) & (at_z + d < nz) for d in (-2, -1, 0, 1, 2)}
            for t in range(tiles):
                at_y = me_y * ny + t * 8 + row8
                ok_y = {
                    d: (at_y + d >= 0) & (at_y + d < splits * ny) for d in (-2, -1, 0, 1, 2)
                }
                words = [
                    mask_ref[w, x, t * 8 : t * 8 + 8, h * LANES : (h + 1) * LANES]
                    for w in range(4)
                ]
                for n, (dx, dy, dz) in enumerate(OFFSETS):
                    squared = dx * dx + dy * dy + dz * dz
                    scale = bond_stiffness / squared
                    if squared == 4:
                        scale = scale * 2.0
                    ok = ((words[n // 8] & (1 << (n % 8))) != 0) & ok_y[dy] & ok_z[dz]
                    factors[n, x, h, t * 8 : t * 8 + 8, :] = jnp.where(
                        ok, scale * ok_x[dx], 0.0
                    )
        for c in range(3):
            for h in range(halves):
                zs = slice(h * LANES, (h + 1) * LANES)
                out_vel[c, x, :, zs] = vel_ref[c, x, :, zs]
                out_disp[c, x, :, zs] = disp_ref[c, x, :, zs]
                force[c, x, h] = acc_ref[c, x, :, zs]

    for r in range(per_group):
        qp[r] = qpos_ref[mine_ref[r]]
        qv[r] = qvel_ref[mine_ref[r]]
        qa[r] = qacc_ref[mine_ref[r]]
    slot_point[slots] = jnp.zeros(slot_point.shape[1:], jnp.float32)
    slot_part[slots] = jnp.zeros(slot_part.shape[1:], jnp.float32)

    count = groups - 1
    for dx, dy in SIDES + CORNERS:
        count = count + jnp.where(exists(dx, dy), 1, 0)
    pl.semaphore_wait(barrier, count)

    def shifted(parts, by):
        rows = parts[0].shape[0]
        lanes = lax.broadcasted_iota(jnp.int32, (rows, LANES), 1)
        rolled = [pltpu.roll(p, (-by) % LANES, axis=1) for p in parts]
        out = []
        for h in range(len(parts)):
            other = h + 1 if by > 0 else h - 1
            if 0 <= other < len(parts):
                edge = lanes >= LANES - by if by > 0 else lanes < -by
                out.append(jnp.where(edge, rolled[other], rolled[h]))
            else:
                out.append(rolled[h])
        return out

    def put(c, x, rows, parts, shifts=True):
        for h, p in enumerate(parts):
            u_0[c, x, h, rows, :] = p
        if shifts:
            for ref, by in ((u_p, 1), (u_m, -1)):
                for h, p in enumerate(shifted(parts, by)):
                    ref[c, x, h, rows, :] = p + float(by) if c == 2 else p

    def copy_side(s, k, dx):
        src = u_0.at[:, 2:4, :, 8 : 8 + ny, :] if dx < 0 else u_0.at[:, nx : nx + 2, :, 8 : 8 + ny, :]
        return pltpu.make_async_remote_copy(
            src_ref=src, dst_ref=got_x.at[s, k], send_sem=send_x.at[s, k],
            recv_sem=recv_x.at[s, k], device_id=(me_x + dx, me_y), device_id_type=MESH,
        )

    def copy_edge(s, k, dy):
        return pltpu.make_async_remote_copy(
            src_ref=edges_y.at[s, k], dst_ref=got_y.at[s, k], send_sem=send_y.at[s, k],
            recv_sem=recv_y.at[s, k], device_id=(me_x, me_y + dy), device_id_type=MESH,
        )

    def copy_corner(s, k, dx, dy):
        return pltpu.make_async_remote_copy(
            src_ref=edges_c.at[s, k], dst_ref=got_c.at[s, k], send_sem=send_c.at[s, k],
            recv_sem=recv_c.at[s, k], device_id=(me_x + dx, me_y + dy), device_id_type=MESH,
        )

    def copy_part(s, p, flip_x, flip_y):
        px = me_x + (1 - 2 * my_x) * flip_x
        py = me_y + (1 - 2 * my_y) * flip_y
        return pltpu.make_async_remote_copy(
            src_ref=part_send.at[s], dst_ref=part_got.at[s, my_id], send_sem=send_p.at[s, p],
            recv_sem=recv_p.at[s, p], device_id=(px, py), device_id_type=MESH,
        )

    def copy_group(g):
        x, y = group_xy(g)
        return pltpu.make_async_remote_copy(
            src_ref=fin, dst_ref=gathered.at[my_group], send_sem=send_g.at[g],
            recv_sem=recv_g.at[my_group], device_id=(x, y), device_id_type=MESH,
        )

    def take_group(g):
        x, y = group_xy(g)
        return pltpu.make_async_remote_copy(
            src_ref=fin, dst_ref=gathered.at[g], send_sem=send_g.at[g],
            recv_sem=recv_g.at[g], device_id=(x, y), device_id_type=MESH,
        )

    partners = ((0, 1), (1, 0), (1, 1))

    def substep(s):
        @pl.loop(0, nx)
        def _(x):
            for c in range(3):
                parts = []
                for h in range(halves):
                    zs = slice(h * LANES, (h + 1) * LANES)
                    half = out_vel[c, x, :, zs] + 0.5 * time_step * force[c, x, h]
                    out_vel[c, x, :, zs] = half
                    moved = out_disp[c, x, :, zs] + time_step * half
                    out_disp[c, x, :, zs] = moved
                    if c == 0:
                        moved = moved + (x - mid_x).astype(jnp.float32)
                    elif c == 1:
                        rows = lax.broadcasted_iota(jnp.int32, (ny, LANES), 0)
                        moved = moved + (rows - mid_y).astype(jnp.float32)
                    parts.append(moved)
                put(c, x + 2, slice(8, 8 + ny), parts)
                for h, p in enumerate(parts):
                    edges_y[s, 0, c, x, h] = p[0:2]
                    edges_y[s, 1, c, x, h] = p[ny - 2 : ny]
                if c == 2:
                    for ref, by in ((u_pp, 2), (u_mm, -2)):
                        for h, p in enumerate(shifted(parts, by)):
                            ref[x, h] = p + float(by)

        for k, (dx, dy) in enumerate(CORNERS):
            x = 2 if dx < 0 else nx + 1
            y = 8 if dy < 0 else ny + 7
            for c in range(3):
                for h in range(halves):
                    edges_c[s, k, c, h] = u_0[c, x, h, y : y + 1, :]

        for k, d in enumerate((1, -1)):
            @pl.when(exists(d, 0))
            def _():
                copy_side(s, k, d).start()
        for k, d in enumerate((1, -1)):
            @pl.when(exists(0, d))
            def _():
                pltpu.make_async_remote_copy(
                    src_ref=edges_y.at[s, 1 - k], dst_ref=got_y.at[s, k],
                    send_sem=send_y.at[s, k], recv_sem=recv_y.at[s, k],
                    device_id=(me_x, me_y + d), device_id_type=MESH,
                ).start()
        for k, (dx, dy) in enumerate(CORNERS):
            @pl.when(exists(dx, dy))
            def _():
                copy_corner(s, k, dx, dy).start()

        for r in range(per_group):
            half = qv[r] + 0.5 * time_step * qa[r]
            qv[r] = half
            moved = qp[r] + time_step * half
            qp[r] = moved
            for c, base in enumerate(
                ((me_x * nx + mid_x).astype(jnp.float32),
                 (me_y * ny + mid_y).astype(jnp.float32), float(nz - SL))
            ):
                rel[r, c : c + 1] = moved[c : c + 1] - base

        @pl.loop(0, nx)
        def _(x):
            for c in range(3):
                for t in range(tiles):
                    tile = u_0[c, x + 2, top, 8 + 8 * t : 16 + 8 * t, :]
                    for z in range(SL):
                        col = tile[:, LANES - SL + z : LANES - SL + z + 1]
                        if c == 2:
                            col = col + float(z)
                        wide[x, c, z * tiles + t] = jnp.broadcast_to(col, (8, LANES))

        @pl.loop(0, slots)
        def _(k):
            block = targets_ref[s * slots + k]
            slot = slots_ref[s * slots + k]
            q = rel[slot]
            qs = [jnp.broadcast_to(q[c : c + 1], (8, LANES)) for c in range(3)]
            sums = [zero_tile] * 3
            for t in range(tiles):
                outs = [zero_tile] * 3
                for z in range(SL):
                    r = [wide[block, c, z * tiles + t] - qs[c] for c in range(3)]
                    sq = r[0] * r[0] + r[1] * r[1] + r[2] * r[2]
                    w = contact_stiffness * jnp.exp(sq * (-1.0 / contact_width))
                    for c in range(3):
                        pulled = w * r[c]
                        sums[c] = sums[c] + pulled
                        total = jnp.sum(pulled, axis=1, keepdims=True)
                        outs[c] = jnp.where(lane == LANES - SL + z, total, outs[c])
                for c in range(3):
                    slot_point[k, c, t * 8 : t * 8 + 8, :] = outs[c]
            for c in range(3):
                slot_part[k, c] = sums[c]

        for g in range(per_group):
            for c in range(3):
                total = zero_tile
                for x in range(nx):
                    total = total + slot_part[inverse_ref[(s * nx + x) * per_group + g], c]
                total = -jnp.sum(total, axis=0, keepdims=True)
                part_send[s, g, c : c + 1] = total
                part_got[s, my_id, g, c : c + 1] = total
        for p, (fx, fy) in enumerate(partners):
            copy_part(s, p, fx, fy).start()

        for k, d in enumerate((-1, 1)):
            @pl.when(exists(d, 0))
            def _():
                pltpu.make_async_remote_copy(
                    src_ref=got_x.at[s, k], dst_ref=got_x.at[s, k], send_sem=send_x.at[s, k],
                    recv_sem=recv_x.at[s, k], device_id=(me_x + d, me_y), device_id_type=MESH,
                ).wait_recv()
                for layer in range(2):
                    x = layer if d < 0 else nx + 2 + layer
                    near = layer == (1 if d < 0 else 0)
                    for c in range(3):
                        parts = [got_x[s, k, c, layer, h] for h in range(halves)]
                        if c == 0:
                            parts = [p + float(d * nx) for p in parts]
                        put(c, x, slice(8, 8 + ny), parts, near)
        for k, d in enumerate((-1, 1)):
            @pl.when(exists(0, d))
            def _():
                pltpu.make_async_remote_copy(
                    src_ref=got_y.at[s, k], dst_ref=got_y.at[s, k], send_sem=send_y.at[s, k],
                    recv_sem=recv_y.at[s, k], device_id=(me_x, me_y + d), device_id_type=MESH,
                ).wait_recv()

                @pl.loop(0, nx)
                def _(x):
                    for c in range(3):
                        parts = [got_y[s, k, c, x, h] for h in range(halves)]
                        if c == 1:
                            parts = [p + float(d * ny) for p in parts]
                        y = 6 if d < 0 else ny + 8
                        put(c, x + 2, slice(y, y + 2), parts)
        for k, (dx, dy) in enumerate(CORNERS):
            j = CORNERS.index((-dx, -dy))

            @pl.when(exists(dx, dy))
            def _():
                pltpu.make_async_remote_copy(
                    src_ref=got_c.at[s, j], dst_ref=got_c.at[s, j], send_sem=send_c.at[s, j],
                    recv_sem=recv_c.at[s, j], device_id=(me_x + dx, me_y + dy),
                    device_id_type=MESH,
                ).wait_recv()
                x = 1 if dx < 0 else nx + 2
                y = 7 if dy < 0 else ny + 8
                for c in range(3):
                    parts = [got_c[s, j, c, h] for h in range(halves)]
                    if c == 0:
                        parts = [p + float(dx * nx) for p in parts]
                    if c == 1:
                        parts = [p + float(dy * ny) for p in parts]
                    put(c, x, slice(y, y + 1), parts)

        @pl.loop(0, nx)
        def _(x):
            for h in range(halves):
                for t in range(tiles):
                    rows = slice(8 * t, 8 * t + 8)
                    own = [u_0[c, x + 2, h, 8 + 8 * t : 16 + 8 * t, :] for c in range(3)]
                    total = [None, None, None]
                    for n, (dx, dy, dz) in enumerate(OFFSETS):
                        length = math.sqrt(dx * dx + dy * dy + dz * dz)
                        y0 = 8 + 8 * t + dy
                        if abs(dz) == 2:
                            by = 2 if dz > 0 else -2
                            near = [
                                shifted([u_0[c, x + 2, i, y0 : y0 + 8, :] for i in range(halves)], by)[h]
                                for c in range(2)
                            ] + [(u_pp if dz > 0 else u_mm)[x, h, rows, :]]
                        else:
                            ref = {0: u_0, 1: u_p, -1: u_m}[dz]
                            near = [ref[c, x + 2 + dx, h, y0 : y0 + 8, :] for c in range(3)]
                        d = [near[c] - own[c] for c in range(3)]
                        q = d[0] * d[0] + d[1] * d[1] + d[2] * d[2]
                        root = q * lax.rsqrt(jnp.maximum(q, tiny))
                        coefficient = (root - length) * factors[n, x, h, rows, :]
                        for c, e in enumerate((dx, dy, dz)):
                            if e:
                                if total[c] is None:
                                    total[c] = coefficient if e > 0 else -coefficient
                                elif e > 0:
                                    total[c] = total[c] + coefficient
                                else:
                                    total[c] = total[c] - coefficient
                    zs = slice(h * LANES, (h + 1) * LANES)
                    for c in range(3):
                        f = total[c]
                        if h == top:
                            for g in range(per_group):
                                f = f + slot_point[inverse_ref[(s * nx + x) * per_group + g], c, rows, :]
                        force[c, x, h, rows, :] = f
                        out_vel[c, x, rows, zs] = out_vel[c, x, rows, zs] + 0.5 * time_step * f

        for p, (fx, fy) in enumerate(partners):
            ix = my_x + (1 - 2 * my_x) * fx
            iy = my_y + (1 - 2 * my_y) * fy
            pltpu.make_async_remote_copy(
                src_ref=part_send.at[s], dst_ref=part_got.at[s, ix * 2 + iy],
                send_sem=send_p.at[s, p], recv_sem=recv_p.at[s, p],
                device_id=(me_x + ix - my_x, me_y + iy - my_y), device_id_type=MESH,
            ).wait()
        for r in range(per_group):
            total = part_got[s, 0, r] + part_got[s, 1, r] + part_got[s, 2, r] + part_got[s, 3, r]
            total = inverse_mass * total
            qa[r] = total
            qv[r] = qv[r] + 0.5 * time_step * total

        for k, d in enumerate((1, -1)):
            @pl.when(exists(d, 0))
            def _():
                copy_side(s, k, d).wait_send()

            @pl.when(exists(0, d))
            def _():
                pltpu.make_async_remote_copy(
                    src_ref=edges_y.at[s, 1 - k], dst_ref=got_y.at[s, k],
                    send_sem=send_y.at[s, k], recv_sem=recv_y.at[s, k],
                    device_id=(me_x, me_y + d), device_id_type=MESH,
                ).wait_send()
        for k, (dx, dy) in enumerate(CORNERS):
            @pl.when(exists(dx, dy))
            def _():
                copy_corner(s, k, dx, dy).wait_send()

    @pl.loop(0, subs)
    def _(s):
        substep(s)

    for r in range(per_group):
        for i, ref in enumerate((qp, qv)):
            fin[r, i] = ref[r]
            gathered[my_group, r, i] = ref[r]

    @pl.loop(0, groups)
    def _(g):
        @pl.when(g != my_group)
        def _():
            copy_group(g).start()

    @pl.loop(0, groups)
    def _(g):
        @pl.when(g != my_group)
        def _():
            take_group(g).wait()

    @pl.loop(0, blocks)
    def _(b):
        where = place_ref[b]
        out_pos[b] = gathered[where // per_group, lax.rem(where, per_group), 0]
        out_pvel[b] = gathered[where // per_group, lax.rem(where, per_group), 1]


def per_device(
    slabs, splits,
    displacement, velocity, acceleration, bond_masks, proj_pos, proj_vel, proj_acc, contact_pairs
):
    _, nx, ny, nz = displacement.shape
    subs = contact_pairs.shape[0]
    slots = contact_pairs.shape[2]
    blocks = proj_pos.shape[0]
    groups = (slabs // 2) * (splits // 2)
    per_group = blocks // groups
    halves = nz // LANES
    assert nx == SB_DEV and ny * SL == PTS and ny % 8 == 0

    middle = jnp.mean(proj_pos[:, :2, :], axis=2)
    gx = jnp.clip(jnp.floor((middle[:, 0] + 0.5) / (2 * nx)).astype(jnp.int32), 0, slabs // 2 - 1)
    gy = jnp.clip(jnp.floor((middle[:, 1] + 0.5) / (2 * ny)).astype(jnp.int32), 0, splits // 2 - 1)
    group = gx * (splits // 2) + gy
    number = jnp.arange(blocks)
    rank = jnp.sum(
        ((group[:, None] == group[None, :]) & (number[None, :] < number[:, None])).astype(jnp.int32),
        axis=1,
    )
    place = jnp.minimum(rank, per_group - 1) + group * per_group
    my_group = (lax.axis_index("slab") // 2) * (splits // 2) + lax.axis_index("split") // 2
    wanted = my_group * per_group + jnp.arange(per_group)
    mine = jnp.max(jnp.where(place[None, :] == wanted[:, None], number[None, :], 0), axis=1)
    targets = contact_pairs[:, 0]
    chosen = contact_pairs[:, 1]
    slot = jnp.max(
        jnp.where(chosen[:, :, None] == mine[None, None, :], jnp.arange(per_group), 0), axis=2
    )
    hit = (
        (targets[:, None, None, :] == jnp.arange(nx)[None, :, None, None])
        & (chosen[:, None, None, :] == mine[None, None, :, None])
    )
    inverse = jnp.min(jnp.where(hit, jnp.arange(slots), slots), axis=3)

    dims = (subs, nx, ny, nz, slabs, splits, per_group, blocks)
    f32 = jnp.float32
    smem = pl.BlockSpec(memory_space=pltpu.SMEM)
    vmem = pl.BlockSpec(memory_space=pltpu.VMEM)
    padded = (3, nx + 4, halves, ny + 16, LANES)
    dma = pltpu.SemaphoreType.DMA
    scratch = [
        pltpu.VMEM(padded, f32),
        pltpu.VMEM(padded, f32),
        pltpu.VMEM(padded, f32),
        pltpu.VMEM((nx, halves, ny, LANES), f32),
        pltpu.VMEM((nx, halves, ny, LANES), f32),
        pltpu.VMEM((3, nx, halves, ny, LANES), f32),
        pltpu.VMEM((32, nx, halves, ny, LANES), f32),
        pltpu.VMEM((subs, 2, 3, nx, halves, 2, LANES), f32),
        pltpu.VMEM((subs, 4, 3, halves, 1, LANES), f32),
        pltpu.VMEM((subs, 2, 3, 2, halves, ny, LANES), f32),
        pltpu.VMEM((subs, 2, 3, nx, halves, 2, LANES), f32),
        pltpu.VMEM((subs, 4, 3, halves, 1, LANES), f32),
        pltpu.VMEM((nx, 3, ny // 8 * SL, 8, LANES), f32),
        pltpu.VMEM((slots + 1, 3, ny, LANES), f32),
        pltpu.VMEM((slots + 1, 3, 8, LANES), f32),
        pltpu.VMEM((per_group, 3, PTS), f32),
        pltpu.VMEM((per_group, 3, PTS), f32),
        pltpu.VMEM((per_group, 3, PTS), f32),
        pltpu.VMEM((per_group, 3, PTS), f32),
        pltpu.VMEM((subs, per_group, 3, PTS), f32),
        pltpu.VMEM((subs, 4, per_group, 3, PTS), f32),
        pltpu.VMEM((per_group, 2, 3, PTS), f32),
        pltpu.VMEM((groups, per_group, 2, 3, PTS), f32),
        dma((subs, 2)), dma((subs, 2)), dma((subs, 2)), dma((subs, 2)),
        dma((subs, 4)), dma((subs, 4)), dma((subs, 3)), dma((subs, 3)),
        dma((groups,)), dma((groups,)),
    ]
    return pl.pallas_call(
        functools.partial(kernel, dims),
        out_shape=(
            jax.ShapeDtypeStruct(displacement.shape, f32),
            jax.ShapeDtypeStruct(displacement.shape, f32),
            jax.ShapeDtypeStruct(proj_pos.shape, f32),
            jax.ShapeDtypeStruct(proj_pos.shape, f32),
        ),
        in_specs=[smem] * 5 + [vmem] * 7,
        out_specs=(vmem,) * 4,
        scratch_shapes=scratch,
        compiler_params=pltpu.CompilerParams(
            collective_id=0, has_side_effects=True, vmem_limit_bytes=60 * 1024 * 1024
        ),
    )(
        targets.reshape(-1), slot.reshape(-1), inverse.reshape(-1), mine, place,
        displacement, velocity, acceleration, bond_masks, proj_pos, proj_vel, proj_acc,
    )


def solution(mesh):
    cells = P(None, "slab", "split", None)
    return jax.shard_map(
        functools.partial(per_device, mesh.shape["slab"], mesh.shape["split"]),
        mesh=mesh,
        in_specs=(cells, cells, cells, cells, P(), P(), P(), P(None, None, ("slab", "split"))),
        out_specs=(cells, cells, P(), P()),
        check_vma=False,
    )
```

```python
import functools
import math

import jax
import jax.numpy as jnp
from jax import lax
from jax.experimental import pallas as pl
from jax.experimental.pallas import tpu as pltpu
from jax.sharding import PartitionSpec as P

SL = 4
PTS = 128
SB_DEV = 8
LANES = 128

time_step = 0.25
bond_stiffness = 0.5
contact_stiffness = 0.05
contact_width = 8.0
inverse_mass = 0.5
tiny = 1e-30
MESH = pl.DeviceIdType.MESH


def bond_offsets():
    listed = []
    for shift_x in (-2, -1, 0, 1, 2):
        for shift_y in (-2, -1, 0, 1, 2):
            for shift_z in (-2, -1, 0, 1, 2):
                squared = shift_x * shift_x + shift_y * shift_y + shift_z * shift_z
                if 0 < squared <= 4:
                    listed.append((shift_x, shift_y, shift_z))
    return listed


OFFSETS = bond_offsets()
CORNERS = [(-1, -1), (-1, 1), (1, -1), (1, 1)]
SIDES = [(-1, 0), (1, 0), (0, -1), (0, 1)]


def kernel(
    dims,
    targets_ref, slots_ref, inverse_ref, mine_ref, place_ref,
    disp_hbm, vel_hbm, acc_hbm, mask_hbm, qpos_ref, qvel_ref, qacc_ref,
    out_disp, out_vel, out_pos, out_pvel,
    u_0, u_p, u_m, u_pp, u_mm, force, still, mask_ref, in_sem, factors, edges_y, edges_c,
    got_x, got_y, got_c, wide, slot_point, slot_part, qp, qv, qa, rel,
    part_send, part_got, fin, gathered,
    send_x, recv_x, send_y, recv_y, send_c, recv_c, send_p, recv_p, send_g, recv_g,
):
    subs, nx, ny, nz, slabs, splits, per_group, blocks = dims
    halves = nz // LANES
    tiles = ny // 8
    slots = slots_ref.shape[1]
    top = halves - 1
    me_x = lax.axis_index("slab")
    me_y = lax.axis_index("split")
    mid_x, mid_y = nx // 2, ny // 2
    half_split = splits // 2
    groups = (slabs // 2) * half_split
    my_group = (me_x // 2) * half_split + me_y // 2
    my_x, my_y = lax.rem(me_x, 2), lax.rem(me_y, 2)
    my_id = my_x * 2 + my_y

    def exists(dx, dy):
        ok = None
        for d, me, n in ((dx, me_x, slabs), (dy, me_y, splits)):
            if d:
                cond = (me > 0) if d < 0 else (me < n - 1)
                ok = cond if ok is None else ok & cond
        return ok

    loads = [
        pltpu.make_async_copy(src, dst, in_sem.at[i])
        for i, (src, dst) in enumerate(
            ((mask_hbm, mask_ref), (acc_hbm, force), (vel_hbm, out_vel), (disp_hbm, out_disp))
        )
    ]
    for load in loads:
        load.start()

    barrier = pltpu.get_barrier_semaphore()

    def greet(x, y):
        pl.semaphore_signal(barrier, inc=1, device_id=(x, y), device_id_type=MESH)

    for dx, dy in SIDES + CORNERS:
        @pl.when(exists(dx, dy))
        def _():
            greet(me_x + dx, me_y + dy)

    def group_xy(g):
        return 2 * (g // half_split) + my_x, 2 * lax.rem(g, half_split) + my_y

    @pl.loop(0, groups)
    def _(g):
        @pl.when(g != my_group)
        def _():
            x, y = group_xy(g)
            greet(x, y)

    lane = lax.broadcasted_iota(jnp.int32, (8, LANES), 1)
    row8 = lax.broadcasted_iota(jnp.int32, (8, LANES), 0)

    zero_tile = jnp.zeros((8, LANES), jnp.float32)
    for ref in (u_0, u_p, u_m):
        for x in (0, 1, nx + 2, nx + 3):
            ref[:, x] = jnp.zeros(ref.shape[:1] + ref.shape[2:], jnp.float32)

        @pl.loop(2, nx + 2)
        def _(x):
            for c in range(3):
                for h in range(halves):
                    ref[c, x, h, 0:8, :] = zero_tile
                    ref[c, x, h, ny + 8 : ny + 16, :] = zero_tile

    loads[0].wait()

    @pl.loop(0, nx)
    def _(x):
        at_x = me_x * nx + x
        ok_x = {
            d: jnp.where((at_x + d >= 0) & (at_x + d < slabs * nx), 1.0, 0.0)
            for d in (-2, -1, 0, 1, 2)
        }
        for h in range(halves):
            at_z = lane + h * LANES
            ok_z = {d: (at_z + d >= 0) & (at_z + d < nz) for d in (-2, -1, 0, 1, 2)}
            for t in range(tiles):
                at_y = me_y * ny + t * 8 + row8
                ok_y = {
                    d: (at_y + d >= 0) & (at_y + d < splits * ny) for d in (-2, -1, 0, 1, 2)
                }
                words = [
                    mask_ref[w, x, t * 8 : t * 8 + 8, h * LANES : (h + 1) * LANES]
                    for w in range(4)
                ]
                rest = [[zero_tile] * 3 for _ in range(4)]
                for n, (dx, dy, dz) in enumerate(OFFSETS):
                    squared = dx * dx + dy * dy + dz * dz
                    scale = bond_stiffness / squared
                    if squared == 4:
                        scale = scale * 2.0
                    ok = ((words[n // 8] & (1 << (n % 8))) != 0) & ok_y[dy] & ok_z[dz]
                    factor = jnp.where(ok, scale * ok_x[dx], 0.0)
                    factors[n, x, h, t * 8 : t * 8 + 8, :] = factor
                    kind = squared - 1
                    for c, e in enumerate((dx, dy, dz)):
                        if e > 0:
                            rest[kind][c] = rest[kind][c] + factor
                        elif e:
                            rest[kind][c] = rest[kind][c] - factor
                for c in range(3):
                    still[c, x, t * 8 : t * 8 + 8, h * LANES : (h + 1) * LANES] = (
                        rest[0][c] + math.sqrt(2.0) * rest[1][c]
                        + math.sqrt(3.0) * rest[2][c] + 2.0 * rest[3][c]
                    )

    for r in range(per_group):
        for c in range(3):
            qp[r, c : c + 1] = qpos_ref[c, pl.ds(mine_ref[r], 1)]
            qv[r, c : c + 1] = qvel_ref[c, pl.ds(mine_ref[r], 1)]
            qa[r, c : c + 1] = qacc_ref[c, pl.ds(mine_ref[r], 1)]
    slot_point[slots] = jnp.zeros(slot_point.shape[1:], jnp.float32)
    slot_part[slots] = jnp.zeros(slot_part.shape[1:], jnp.float32)

    count = groups - 1
    for dx, dy in SIDES + CORNERS:
        count = count + jnp.where(exists(dx, dy), 1, 0)
    pl.semaphore_wait(barrier, count)
    for load in loads[1:]:
        load.wait()

    def shifted(parts, by):
        rows = parts[0].shape[0]
        lanes = lax.broadcasted_iota(jnp.int32, (rows, LANES), 1)
        rolled = [pltpu.roll(p, (-by) % LANES, axis=1) for p in parts]
        out = []
        for h in range(len(parts)):
            other = h + 1 if by > 0 else h - 1
            if 0 <= other < len(parts):
                edge = lanes >= LANES - by if by > 0 else lanes < -by
                out.append(jnp.where(edge, rolled[other], rolled[h]))
            else:
                out.append(rolled[h])
        return out

    def put(c, x, rows, parts, shifts=True):
        for h, p in enumerate(parts):
            u_0[c, x, h, rows, :] = p
        if shifts:
            for ref, by in ((u_p, 1), (u_m, -1)):
                for h, p in enumerate(shifted(parts, by)):
                    ref[c, x, h, rows, :] = p + float(by) if c == 2 else p

    def copy_side(s, k, dx):
        src = u_0.at[:, 2:4, :, 8 : 8 + ny, :] if dx < 0 else u_0.at[:, nx : nx + 2, :, 8 : 8 + ny, :]
        return pltpu.make_async_remote_copy(
            src_ref=src, dst_ref=got_x.at[s, k], send_sem=send_x.at[s, k],
            recv_sem=recv_x.at[s, k], device_id=(me_x + dx, me_y), device_id_type=MESH,
        )

    def copy_corner(s, k, dx, dy):
        return pltpu.make_async_remote_copy(
            src_ref=edges_c.at[s, k], dst_ref=got_c.at[s, k], send_sem=send_c.at[s, k],
            recv_sem=recv_c.at[s, k], device_id=(me_x + dx, me_y + dy), device_id_type=MESH,
        )

    def copy_part(s, p, flip_x, flip_y):
        px = me_x + (1 - 2 * my_x) * flip_x
        py = me_y + (1 - 2 * my_y) * flip_y
        return pltpu.make_async_remote_copy(
            src_ref=part_send.at[s], dst_ref=part_got.at[s, my_id], send_sem=send_p.at[s, p],
            recv_sem=recv_p.at[s, p], device_id=(px, py), device_id_type=MESH,
        )

    def copy_group(g):
        x, y = group_xy(g)
        return pltpu.make_async_remote_copy(
            src_ref=fin, dst_ref=gathered.at[my_group], send_sem=send_g.at[g],
            recv_sem=recv_g.at[my_group], device_id=(x, y), device_id_type=MESH,
        )

    def take_group(g):
        x, y = group_xy(g)
        return pltpu.make_async_remote_copy(
            src_ref=fin, dst_ref=gathered.at[g], send_sem=send_g.at[g],
            recv_sem=recv_g.at[g], device_id=(x, y), device_id_type=MESH,
        )

    partners = ((0, 1), (1, 0), (1, 1))

    def substep(s):
        @pl.loop(0, nx, unroll=2)
        def _(x):
            for c in range(3):
                parts = []
                for h in range(halves):
                    zs = slice(h * LANES, (h + 1) * LANES)
                    half = out_vel[c, x, :, zs] + 0.5 * time_step * force[c, x, :, zs]
                    out_vel[c, x, :, zs] = half
                    moved = out_disp[c, x, :, zs] + time_step * half
                    out_disp[c, x, :, zs] = moved
                    if c == 0:
                        moved = moved + (x - mid_x).astype(jnp.float32)
                    elif c == 1:
                        rows = lax.broadcasted_iota(jnp.int32, (ny, LANES), 0)
                        moved = moved + (rows - mid_y).astype(jnp.float32)
                    parts.append(moved)
                put(c, x + 2, slice(8, 8 + ny), parts)
                for h, p in enumerate(parts):
                    edges_y[s, 0, c, x, h] = p[0:2]
                    edges_y[s, 1, c, x, h] = p[ny - 2 : ny]
                if c == 2:
                    for ref, by in ((u_pp, 2), (u_mm, -2)):
                        for h, p in enumerate(shifted(parts, by)):
                            ref[x, h] = p + float(by)

        for k, (dx, dy) in enumerate(CORNERS):
            x = 2 if dx < 0 else nx + 1
            y = 8 if dy < 0 else ny + 7
            for c in range(3):
                for h in range(halves):
                    edges_c[s, k, c, h] = u_0[c, x, h, y : y + 1, :]

        for k, d in enumerate((1, -1)):
            @pl.when(exists(0, d))
            def _():
                pltpu.make_async_remote_copy(
                    src_ref=edges_y.at[s, 1 - k], dst_ref=got_y.at[s, k],
                    send_sem=send_y.at[s, k], recv_sem=recv_y.at[s, k],
                    device_id=(me_x, me_y + d), device_id_type=MESH,
                ).start()
        for k, (dx, dy) in enumerate(CORNERS):
            @pl.when(exists(dx, dy))
            def _():
                copy_corner(s, k, dx, dy).start()

        for k, d in enumerate((1, -1)):
            @pl.when(exists(d, 0))
            def _():
                copy_side(s, k, d).start()

        for r in range(per_group):
            half = qv[r] + 0.5 * time_step * qa[r]
            qv[r] = half
            moved = qp[r] + time_step * half
            qp[r] = moved
            for c, base in enumerate(
                ((me_x * nx + mid_x).astype(jnp.float32),
                 (me_y * ny + mid_y).astype(jnp.float32), float(nz - SL))
            ):
                rel[r, c : c + 1] = moved[c : c + 1] - base

        @pl.loop(0, nx, unroll=4)
        def _(x):
            for c in range(3):
                for t in range(tiles):
                    tile = u_0[c, x + 2, top, 8 + 8 * t : 16 + 8 * t, :]
                    for z in range(SL):
                        col = tile[:, LANES - SL + z : LANES - SL + z + 1]
                        if c == 2:
                            col = col + float(z)
                        wide[x, c, z * tiles + t] = jnp.broadcast_to(col, (8, LANES))

        @pl.loop(0, slots, unroll=4)
        def _(k):
            block = targets_ref[s, k]
            slot = slots_ref[s, k]
            q = rel[slot]
            qs = [jnp.broadcast_to(q[c : c + 1], (8, LANES)) for c in range(3)]
            sums = [zero_tile] * 3
            for t in range(tiles):
                outs = [zero_tile] * 3
                for z in range(SL):
                    r = [wide[block, c, z * tiles + t] - qs[c] for c in range(3)]
                    sq = r[0] * r[0] + r[1] * r[1] + r[2] * r[2]
                    w = contact_stiffness * jnp.exp(sq * (-1.0 / contact_width))
                    for c in range(3):
                        pulled = w * r[c]
                        sums[c] = sums[c] + pulled
                        total = jnp.sum(pulled, axis=1, keepdims=True)
                        outs[c] = jnp.where(lane == LANES - SL + z, total, outs[c])
                for c in range(3):
                    slot_point[k, c, t * 8 : t * 8 + 8, :] = outs[c]
            for c in range(3):
                slot_part[k, c] = sums[c]

        for g in range(per_group):
            for c in range(3):
                total = zero_tile
                for x in range(nx):
                    total = total + slot_part[inverse_ref[s, x * per_group + g], c]
                total = -jnp.sum(total, axis=0, keepdims=True)
                part_send[s, g, c : c + 1] = total
                part_got[s, my_id, g, c : c + 1] = total
        for p, (fx, fy) in enumerate(partners):
            copy_part(s, p, fx, fy).start()

        for k, d in enumerate((-1, 1)):
            @pl.when(exists(0, d))
            def _():
                pltpu.make_async_remote_copy(
                    src_ref=got_y.at[s, k], dst_ref=got_y.at[s, k], send_sem=send_y.at[s, k],
                    recv_sem=recv_y.at[s, k], device_id=(me_x, me_y + d), device_id_type=MESH,
                ).wait_recv()

                @pl.loop(0, nx)
                def _(x):
                    for c in range(3):
                        parts = [got_y[s, k, c, x, h] for h in range(halves)]
                        if c == 1:
                            parts = [p + float(d * ny) for p in parts]
                        y = 6 if d < 0 else ny + 8
                        put(c, x + 2, slice(y, y + 2), parts)
        def bond_layer(x):
            for h in range(halves):
                for t in range(tiles):
                    rows = slice(8 * t, 8 * t + 8)
                    own = [u_0[c, x + 2, h, 8 + 8 * t : 16 + 8 * t, :] for c in range(3)]
                    total = [None, None, None]
                    for n, (dx, dy, dz) in enumerate(OFFSETS):
                        y0 = 8 + 8 * t + dy
                        if abs(dz) == 2:
                            by = 2 if dz > 0 else -2
                            near = [
                                shifted([u_0[c, x + 2, i, y0 : y0 + 8, :] for i in range(halves)], by)[h]
                                for c in range(2)
                            ] + [(u_pp if dz > 0 else u_mm)[x, h, rows, :]]
                        else:
                            ref = {0: u_0, 1: u_p, -1: u_m}[dz]
                            near = [ref[c, x + 2 + dx, h, y0 : y0 + 8, :] for c in range(3)]
                        d = [near[c] - own[c] for c in range(3)]
                        q = d[0] * d[0] + d[1] * d[1] + d[2] * d[2]
                        root = q * lax.rsqrt(jnp.maximum(q, tiny))
                        coefficient = root * factors[n, x, h, rows, :]
                        for c, e in enumerate((dx, dy, dz)):
                            if e:
                                if total[c] is None:
                                    total[c] = coefficient if e > 0 else -coefficient
                                elif e > 0:
                                    total[c] = total[c] + coefficient
                                else:
                                    total[c] = total[c] - coefficient
                    zs = slice(h * LANES, (h + 1) * LANES)
                    for c in range(3):
                        f = total[c] - still[c, x, rows, zs]
                        if h == top:
                            for g in range(per_group):
                                f = f + slot_point[inverse_ref[s, x * per_group + g], c, rows, :]
                        force[c, x, rows, zs] = f
                        out_vel[c, x, rows, zs] = out_vel[c, x, rows, zs] + 0.5 * time_step * f

        @pl.loop(0, nx // 2)
        def _(i):
            bond_layer(i + nx // 4)

        for k, d in enumerate((-1, 1)):
            @pl.when(exists(d, 0))
            def _():
                pltpu.make_async_remote_copy(
                    src_ref=got_x.at[s, k], dst_ref=got_x.at[s, k], send_sem=send_x.at[s, k],
                    recv_sem=recv_x.at[s, k], device_id=(me_x + d, me_y), device_id_type=MESH,
                ).wait_recv()
                for layer in range(2):
                    x = layer if d < 0 else nx + 2 + layer
                    near = layer == (1 if d < 0 else 0)
                    for c in range(3):
                        parts = [got_x[s, k, c, layer, h] for h in range(halves)]
                        if c == 0:
                            parts = [p + float(d * nx) for p in parts]
                        put(c, x, slice(8, 8 + ny), parts, near)
        for k, (dx, dy) in enumerate(CORNERS):
            j = CORNERS.index((-dx, -dy))

            @pl.when(exists(dx, dy))
            def _():
                pltpu.make_async_remote_copy(
                    src_ref=got_c.at[s, j], dst_ref=got_c.at[s, j], send_sem=send_c.at[s, j],
                    recv_sem=recv_c.at[s, j], device_id=(me_x + dx, me_y + dy),
                    device_id_type=MESH,
                ).wait_recv()
                x = 1 if dx < 0 else nx + 2
                y = 7 if dy < 0 else ny + 8
                for c in range(3):
                    parts = [got_c[s, j, c, h] for h in range(halves)]
                    if c == 0:
                        parts = [p + float(dx * nx) for p in parts]
                    if c == 1:
                        parts = [p + float(dy * ny) for p in parts]
                    put(c, x, slice(y, y + 1), parts)

        @pl.loop(0, nx // 2)
        def _(i):
            bond_layer(jnp.where(i < nx // 4, i, i + nx // 2))

        for p, (fx, fy) in enumerate(partners):
            ix = my_x + (1 - 2 * my_x) * fx
            iy = my_y + (1 - 2 * my_y) * fy
            pltpu.make_async_remote_copy(
                src_ref=part_send.at[s], dst_ref=part_got.at[s, ix * 2 + iy],
                send_sem=send_p.at[s, p], recv_sem=recv_p.at[s, p],
                device_id=(me_x + ix - my_x, me_y + iy - my_y), device_id_type=MESH,
            ).wait()
        for r in range(per_group):
            total = part_got[s, 0, r] + part_got[s, 1, r] + part_got[s, 2, r] + part_got[s, 3, r]
            total = inverse_mass * total
            qa[r] = total
            qv[r] = qv[r] + 0.5 * time_step * total

        for k, d in enumerate((1, -1)):
            @pl.when(exists(d, 0))
            def _():
                copy_side(s, k, d).wait_send()

            @pl.when(exists(0, d))
            def _():
                pltpu.make_async_remote_copy(
                    src_ref=edges_y.at[s, 1 - k], dst_ref=got_y.at[s, k],
                    send_sem=send_y.at[s, k], recv_sem=recv_y.at[s, k],
                    device_id=(me_x, me_y + d), device_id_type=MESH,
                ).wait_send()
        for k, (dx, dy) in enumerate(CORNERS):
            @pl.when(exists(dx, dy))
            def _():
                copy_corner(s, k, dx, dy).wait_send()

    @pl.loop(0, subs)
    def _(s):
        substep(s)

    for r in range(per_group):
        for i, ref in enumerate((qp, qv)):
            fin[r, i] = ref[r]
            gathered[my_group, r, i] = ref[r]

    @pl.loop(0, groups)
    def _(g):
        @pl.when(g != my_group)
        def _():
            copy_group(g).start()

    @pl.loop(0, groups)
    def _(g):
        @pl.when(g != my_group)
        def _():
            take_group(g).wait()

    @pl.loop(0, blocks)
    def _(b):
        where = place_ref[b]
        both = [gathered[where // per_group, lax.rem(where, per_group), i] for i in range(2)]
        for c in range(3):
            out_pos[c, pl.ds(b, 1)] = both[0][c : c + 1]
            out_pvel[c, pl.ds(b, 1)] = both[1][c : c + 1]


def finish_kernel(moved_ref, speed_ref, out_moved, out_speed):
    out_moved[...] = moved_ref[...]
    out_speed[...] = speed_ref[...]


def finish(moved, speed):
    block = pl.BlockSpec((1,) + moved.shape[1:], lambda c: (c, 0, 0, 0))
    return pl.pallas_call(
        finish_kernel,
        grid=(moved.shape[0],),
        out_shape=(jax.ShapeDtypeStruct(moved.shape, moved.dtype),) * 2,
        in_specs=[block] * 2,
        out_specs=(block,) * 2,
        compiler_params=pltpu.CompilerParams(vmem_limit_bytes=16 * 1024 * 1024),
    )(moved, speed)


def per_device(
    slabs, splits,
    displacement, velocity, acceleration, bond_masks, proj_pos, proj_vel, proj_acc, contact_pairs
):
    _, nx, ny, nz = displacement.shape
    subs = contact_pairs.shape[0]
    slots = contact_pairs.shape[2]
    blocks = proj_pos.shape[0]
    groups = (slabs // 2) * (splits // 2)
    per_group = blocks // groups
    halves = nz // LANES
    assert nx == SB_DEV and ny * SL == PTS and ny % 8 == 0

    middle = jnp.mean(proj_pos[:, :2, :], axis=2)
    gx = jnp.clip(jnp.floor((middle[:, 0] + 0.5) / (2 * nx)).astype(jnp.int32), 0, slabs // 2 - 1)
    gy = jnp.clip(jnp.floor((middle[:, 1] + 0.5) / (2 * ny)).astype(jnp.int32), 0, splits // 2 - 1)
    group = gx * (splits // 2) + gy
    number = jnp.arange(blocks)
    rank = jnp.sum(
        ((group[:, None] == group[None, :]) & (number[None, :] < number[:, None])).astype(jnp.int32),
        axis=1,
    )
    place = jnp.minimum(rank, per_group - 1) + group * per_group
    my_group = (lax.axis_index("slab") // 2) * (splits // 2) + lax.axis_index("split") // 2
    wanted = my_group * per_group + jnp.arange(per_group)
    mine = jnp.max(jnp.where(place[None, :] == wanted[:, None], number[None, :], 0), axis=1)
    targets = contact_pairs[:, 0]
    chosen = contact_pairs[:, 1]
    slot = jnp.max(
        jnp.where(chosen[:, :, None] == mine[None, None, :], jnp.arange(per_group), 0), axis=2
    )
    pairs = jnp.arange(nx * per_group)
    hit = (targets[:, None, :] == (pairs // per_group)[None, :, None]) & (
        chosen[:, None, :] == jnp.tile(mine, nx)[None, :, None]
    )
    inverse = jnp.min(jnp.where(hit, jnp.arange(slots), slots), axis=2)

    dims = (subs, nx, ny, nz, slabs, splits, per_group, blocks)
    f32 = jnp.float32
    smem = pl.BlockSpec(memory_space=pltpu.SMEM)
    vmem = pl.BlockSpec(memory_space=pltpu.VMEM)
    padded = (3, nx + 4, halves, ny + 16, LANES)
    dma = pltpu.SemaphoreType.DMA
    scratch = [
        pltpu.VMEM(padded, f32),
        pltpu.VMEM(padded, f32),
        pltpu.VMEM(padded, f32),
        pltpu.VMEM((nx, halves, ny, LANES), f32),
        pltpu.VMEM((nx, halves, ny, LANES), f32),
        pltpu.VMEM((3, nx, ny, nz), f32),
        pltpu.VMEM((3, nx, ny, nz), f32),
        pltpu.VMEM((4, nx, ny, nz), jnp.int32),
        pltpu.SemaphoreType.DMA((4,)),
        pltpu.VMEM((32, nx, halves, ny, LANES), f32),
        pltpu.VMEM((subs, 2, 3, nx, halves, 2, LANES), f32),
        pltpu.VMEM((subs, 4, 3, halves, 1, LANES), f32),
        pltpu.VMEM((subs, 2, 3, 2, halves, ny, LANES), f32),
        pltpu.VMEM((subs, 2, 3, nx, halves, 2, LANES), f32),
        pltpu.VMEM((subs, 4, 3, halves, 1, LANES), f32),
        pltpu.VMEM((nx, 3, ny // 8 * SL, 8, LANES), f32),
        pltpu.VMEM((slots + 1, 3, ny, LANES), f32),
        pltpu.VMEM((slots + 1, 3, 8, LANES), f32),
        pltpu.VMEM((per_group, 3, PTS), f32),
        pltpu.VMEM((per_group, 3, PTS), f32),
        pltpu.VMEM((per_group, 3, PTS), f32),
        pltpu.VMEM((per_group, 3, PTS), f32),
        pltpu.VMEM((subs, per_group, 3, PTS), f32),
        pltpu.VMEM((subs, 4, per_group, 3, PTS), f32),
        pltpu.VMEM((per_group, 2, 3, PTS), f32),
        pltpu.VMEM((groups, per_group, 2, 3, PTS), f32),
        dma((subs, 2)), dma((subs, 2)), dma((subs, 2)), dma((subs, 2)),
        dma((subs, 4)), dma((subs, 4)), dma((subs, 3)), dma((subs, 3)),
        dma((groups,)), dma((groups,)),
    ]
    moved, speed, points, point_speed = pl.pallas_call(
        functools.partial(kernel, dims),
        out_shape=(
            jax.ShapeDtypeStruct(displacement.shape, f32),
            jax.ShapeDtypeStruct(displacement.shape, f32),
            jax.ShapeDtypeStruct((3, blocks, PTS), f32),
            jax.ShapeDtypeStruct((3, blocks, PTS), f32),
        ),
        in_specs=[smem] * 5 + [pl.BlockSpec(memory_space=pl.ANY)] * 4 + [vmem] * 3,
        out_specs=(vmem,) * 4,
        scratch_shapes=scratch,
        compiler_params=pltpu.CompilerParams(
            collective_id=0, has_side_effects=True, vmem_limit_bytes=60 * 1024 * 1024
        ),
    )(
        targets, slot, inverse, mine, place,
        displacement, velocity, acceleration, bond_masks,
        jnp.moveaxis(proj_pos, 1, 0), jnp.moveaxis(proj_vel, 1, 0), jnp.moveaxis(proj_acc, 1, 0),
    )
    moved, speed = finish(moved, speed)
    return moved, speed, jnp.moveaxis(points, 0, 1), jnp.moveaxis(point_speed, 0, 1)


def solution(mesh):
    cells = P(None, "slab", "split", None)
    return jax.shard_map(
        functools.partial(per_device, mesh.shape["slab"], mesh.shape["split"]),
        mesh=mesh,
        in_specs=(cells, cells, cells, cells, P(), P(), P(), P(None, None, ("slab", "split"))),
        out_specs=(cells, cells, P(), P()),
        check_vma=False,
    )
```
